32 devices in a mesh: blk: 16 (over z, x, core), rep: 2 (over y).
Axes of the slice: x: 2, y: 2, z: 4, core: 2. Of those that a mesh axis runs over, the one named last changes fastest.
Arguments:
- features: bfloat16 [4096, 128], P(('blk', 'rep')), may hold values from -6 to 6
- tile_mask: int32 [32, 32], P('blk'), may hold values 0 or 1
- multiplicity: int32 [32, 32], P('blk'), may hold values from 1 to 4
- w_query: bfloat16 [128, 128], replicated, may hold values from -0.5 to 0.5
- w_value: bfloat16 [128, 128], replicated, may hold values from -0.5 to 0.5
Outputs:
- updated: bfloat16 [4096, 128], P(('blk', 'rep'))
The draws below stay inside these ranges and needn't reach their ends.
All inputs are finite; a program needn't handle non-finite values. No bound on the sum of `tile_mask` on one device may be relied on, other than what follows from the above.
Results may differ from the reference program's by a relative error of at most 0.0057.
Values may be sent and summed in bfloat16 or wider, within the bound.
A program may use at most 64 MiB of HBM per device.

```python
import jax
import jax.numpy as jnp
from jax import lax

D = 128
TILE = 128
VERTS = 4096
NTILE = 32


def plant(entries, key, smallest, top_value):
    shape = entries.shape
    place = [jax.random.randint(jax.random.fold_in(key, axis), (), 0, shape[axis]) for axis in range(len(shape))]
    entries = entries.at[tuple(place)].set(smallest)
    longest = shape.index(max(shape))
    place[longest] = (place[longest] + 1) % shape[longest]
    return entries.at[tuple(place)].set(top_value)


def level_of(stream_key, extent, split, least, largest):
    def one(position, blocks):
        draws = jax.random.uniform(jax.random.fold_in(jax.random.fold_in(stream_key, 6), position), (blocks,), jnp.float32, least / len(split), largest / len(split))
        return jnp.repeat(jnp.exp(draws), extent[position] // blocks).reshape((-1,) + (1,) * (len(extent) - position - 1))

    factor_of = one(*split[0])
    for cut in split[1:]:
        factor_of = factor_of * one(*cut)
    return factor_of


def gaussian(key, shape, spread, bound, cuts=(), kind=jnp.bfloat16):
    level = level_of(key, shape, cuts, -0.22, 0.18) if cuts else 1.0
    array = jax.random.normal(key, shape, jnp.float32) * spread * level
    return jnp.minimum(jnp.maximum(array, -bound), bound).astype(kind)


def setup_inputs(seed: int = 0) -> dict:
    keys = jax.random.split(jax.random.key(seed), 6)
    return {
        "features": gaussian(keys[0], (VERTS, D), 1.0, 6.0, ((0, 32),)),
        "tile_mask": plant((jax.random.randint(keys[1], (NTILE, NTILE), 0, 2) < 1).astype(jnp.int32), jax.random.fold_in(keys[1], 1), 0, 1),
        "multiplicity": plant(jax.random.randint(keys[2], (NTILE, NTILE), 1, 5), jax.random.fold_in(keys[2], 1), 1, 4).astype(jnp.int32),
        "w_query": gaussian(keys[3], (D, D), D ** -0.5, 0.5),
        "w_value": gaussian(keys[4], (D, D), D ** -0.5, 0.5),
    }


def reference(features, tile_mask, multiplicity, w_query, w_value):
    query = jnp.dot(features, w_query, preferred_element_type=jnp.float32).astype(jnp.bfloat16)
    factor = (tile_mask * multiplicity).astype(jnp.float32)
    block_rows = min(1024, VERTS)
    block_count = VERTS // block_rows
    block_tiles = block_rows // TILE
    query_blocks = query.reshape(block_count, block_rows, D)
    factor_blocks = factor.reshape(block_count, block_tiles, NTILE)
    root_scale = 1.0 / (D ** 0.5)

    def one_block(pieces):
        query_block, factor_block = pieces
        scores = jnp.dot(query_block, features.T, preferred_element_type=jnp.float32) * root_scale
        scores = jnp.where(scores > 0, scores, 0.2 * scores)
        weights = scores.reshape(block_tiles, TILE, NTILE, TILE) * factor_block[:, None, :, None]
        weights = weights.reshape(block_rows, VERTS).astype(jnp.bfloat16)
        return jnp.dot(weights, features, preferred_element_type=jnp.float32)

    summed = lax.map(one_block, (query_blocks, factor_blocks)).reshape(VERTS, D)
    aggregate = (summed * ((2.0 * VERTS) ** -0.5)).astype(jnp.bfloat16)
    mixed = jnp.dot(aggregate, w_value, preferred_element_type=jnp.float32)
    return (features.astype(jnp.float32) + mixed).astype(jnp.bfloat16)
```

```python
import functools
import itertools

import jax
import jax.numpy as jnp
from jax import lax
from jax.experimental import pallas as pl
from jax.experimental.pallas import tpu as pltpu
from jax.sharding import PartitionSpec as P

TILE = 128
MESH = pl.DeviceIdType.MESH


def split_of(blk_count):
    cores = 2 if blk_count % 2 == 0 else 1
    mids = 2 if (blk_count // cores) % 2 == 0 else 1
    return blk_count // (cores * mids), mids, cores


def kernel(
    blk_count, rep_count,
    x_hbm, mask_hbm, mult_hbm, wq_hbm, wv_hbm,
    out_ref,
    tgt, src, masks, mults, wq, wv, factors, weights_acc, sums, sent, got,
    local_sems, tgt_send, tgt_recv, src_send, src_recv, tab_send, tab_recv, sum_send, sum_recv,
):
    fars, mids, cores = split_of(blk_count)
    b = lax.axis_index("blk")
    r = lax.axis_index("rep")
    core = b % cores
    mid = (b // cores) % mids
    far = b // (cores * mids)
    near = list(itertools.product(range(mids), range(cores), range(rep_count)))
    tables = list(itertools.product(range(mids), range(cores)))
    near_count = len(near)

    def near_id(dm, dc, dr):
        m, c, q = (mid + dm) % mids, (core + dc) % cores, (r + dr) % rep_count
        return ((far * mids + m) * cores + c, q)

    def far_id(dh):
        return ((((far + dh) % fars) * mids + mid) * cores + core, r)

    def near_slot(dm, dc, dr):
        return near.index((-dm % mids, -dc % cores, -dr % rep_count))

    barrier = pltpu.get_barrier_semaphore()
    for dh in range(1, fars):
        pl.semaphore_signal(barrier, inc=1, device_id=far_id(dh), device_id_type=MESH)
    for offset in near[1:]:
        pl.semaphore_signal(barrier, inc=1, device_id=near_id(*offset), device_id_type=MESH)
    local = [
        pltpu.make_async_copy(x_hbm, src.at[0], local_sems.at[0]),
        pltpu.make_async_copy(wq_hbm, wq, local_sems.at[1]),
        pltpu.make_async_copy(wv_hbm, wv, local_sems.at[2]),
        pltpu.make_async_copy(mask_hbm, masks.at[0], local_sems.at[3]),
        pltpu.make_async_copy(mult_hbm, mults.at[0], local_sems.at[4]),
    ]
    for copy in local:
        copy.start()
    pl.semaphore_wait(barrier, fars - 1 + near_count - 1)

    copies = []
    for dh in sorted(range(1, fars), key=lambda d: -min(d, fars - d)):
        copies.append(pltpu.make_async_remote_copy(
            src_ref=x_hbm, dst_ref=src.at[-dh % fars],
            send_sem=src_send.at[dh], recv_sem=src_recv.at[-dh % fars],
            device_id=far_id(dh), device_id_type=MESH))
    for k, (dm, dc) in enumerate(tables):
        if k:
            slot = tables.index((-dm % mids, -dc % cores))
            for n, (table, slots) in enumerate(((mask_hbm, masks), (mult_hbm, mults))):
                copies.append(pltpu.make_async_remote_copy(
                    src_ref=table, dst_ref=slots.at[slot],
                    send_sem=tab_send.at[n, k], recv_sem=tab_recv.at[n, slot],
                    device_id=near_id(dm, dc, 0), device_id_type=MESH))
    for k, offset in enumerate(near):
        if k:
            slot = near_slot(*offset)
            copies.append(pltpu.make_async_remote_copy(
                src_ref=x_hbm, dst_ref=tgt.at[slot],
                send_sem=tgt_send.at[k], recv_sem=tgt_recv.at[slot],
                device_id=near_id(*offset), device_id_type=MESH))
    for copy in copies:
        copy.start()

    def arrived(dst, sem):
        pltpu.make_async_copy(dst, dst, sem).wait()

    for copy in local:
        copy.wait()
    root_scale = 1.0 / x_hbm.shape[1] ** 0.5
    width = fars * TILE
    tile_count = masks.shape[2]

    def expand():
        place = lax.broadcasted_iota(jnp.int32, (tile_count, width), 1) // TILE
        f = far + place
        f = jnp.where(f >= fars, f - fars, f)
        tile = ((f * mids + mid) * cores + core) * rep_count + r
        one_hot = (lax.broadcasted_iota(jnp.int32, (tile_count, width), 0) == tile)
        return one_hot.astype(jnp.float32).astype(jnp.bfloat16)

    def query_of(rows):
        return jnp.dot(rows, wq[...], preferred_element_type=jnp.float32).astype(jnp.bfloat16)

    def weigh(query, source, factor):
        score = lax.dot_general(query, source, (((1,), (1,)), ((), ())),
                                preferred_element_type=jnp.float32)
        score = score * factor
        return jnp.maximum(score, 0.2 * score).astype(jnp.bfloat16)

    one_hot = expand()
    for k, (dm, dc) in enumerate(tables):
        if k:
            arrived(masks.at[k], tab_recv.at[0, k])
            arrived(mults.at[k], tab_recv.at[1, k])
        fac = (masks[k] * mults[k]).astype(jnp.float32).astype(jnp.bfloat16)
        wide = jnp.dot(fac, one_hot, preferred_element_type=jnp.float32) * root_scale
        rows = lax.broadcasted_iota(jnp.int32, wide.shape, 0)
        for dr in range(rep_count):
            row = jnp.sum(jnp.where(rows == (r + dr) % rep_count, wide, 0.0), axis=0, keepdims=True)
            factors[near.index((dm, dc, dr))] = row

    own = src[0]
    for k in range(near_count):
        if k:
            arrived(tgt.at[k], tgt_recv.at[k])
            rows = tgt[k]
        else:
            rows = own
        query = query_of(rows)
        weights_acc[k] = query
        sums[k] = jnp.dot(weigh(query, own, factors[k, :, :TILE]), own,
                          preferred_element_type=jnp.float32)

    for dh in range(1, fars):
        arrived(src.at[dh], src_recv.at[dh])
    others = src[1:].reshape(width - TILE, src.shape[2])
    order = sorted(range(near_count), key=lambda k: (k == 0, -sum(v > 0 for v in near[k])))
    for k in order:
        w = weigh(weights_acc[k], others, factors[k, :, TILE:])
        part = sums[k] + jnp.dot(w, others, preferred_element_type=jnp.float32)
        if k:
            sent[k] = part.astype(jnp.bfloat16)
            slot = near_slot(*near[k])
            copy = pltpu.make_async_remote_copy(
                src_ref=sent.at[k], dst_ref=got.at[slot],
                send_sem=sum_send.at[k], recv_sem=sum_recv.at[slot],
                device_id=near_id(*near[k]), device_id_type=MESH)
            copy.start()
            copies.append(copy)
        else:
            total = part
    for k in range(1, near_count):
        arrived(got.at[k], sum_recv.at[k])
        total = total + got[k].astype(jnp.float32)
    verts = TILE * blk_count * rep_count
    aggregate = (total * (2.0 * verts) ** (-0.5)).astype(jnp.bfloat16)
    mixed = jnp.dot(aggregate, wv[...], preferred_element_type=jnp.float32)
    out_ref[...] = (own.astype(jnp.float32) + mixed).astype(jnp.bfloat16)
    for copy in copies:
        copy.wait_send()


def body(blk_count, rep_count, features, tile_mask, multiplicity, w_query, w_value):
    rows, width = features.shape
    assert rows == TILE
    fars, mids, cores = split_of(blk_count)
    near_count = mids * cores * rep_count
    table_rows, table_cols = tile_mask.shape
    dma = pltpu.SemaphoreType.DMA
    return pl.pallas_call(
        functools.partial(kernel, blk_count, rep_count),
        out_shape=jax.ShapeDtypeStruct((rows, width), jnp.bfloat16),
        in_specs=[pl.BlockSpec(memory_space=pl.ANY)] * 5,
        out_specs=pl.BlockSpec(memory_space=pltpu.VMEM),
        scratch_shapes=[
            pltpu.VMEM((near_count, rows, width), jnp.bfloat16),
            pltpu.VMEM((fars, rows, width), jnp.bfloat16),
            pltpu.VMEM((mids * cores, table_rows, table_cols), jnp.int32),
            pltpu.VMEM((mids * cores, table_rows, table_cols), jnp.int32),
            pltpu.VMEM(w_query.shape, jnp.bfloat16),
            pltpu.VMEM(w_value.shape, jnp.bfloat16),
            pltpu.VMEM((near_count, 1, fars * TILE), jnp.float32),
            pltpu.VMEM((near_count, rows, width), jnp.bfloat16),
            pltpu.VMEM((near_count, rows, width), jnp.float32),
            pltpu.VMEM((near_count, rows, width), jnp.bfloat16),
            pltpu.VMEM((near_count, rows, width), jnp.bfloat16),
            dma((5,)),
            dma((near_count,)), dma((near_count,)),
            dma((fars,)), dma((fars,)),
            dma((2, mids * cores)), dma((2, mids * cores)),
            dma((near_count,)), dma((near_count,)),
        ],
        compiler_params=pltpu.CompilerParams(collective_id=0, has_side_effects=True),
    )(features, tile_mask, multiplicity, w_query, w_value)


def solution(mesh):
    in_specs = (P(("blk", "rep"), None), P("blk", None), P("blk", None), P(), P())
    out_specs = P(("blk", "rep"), None)
    run = functools.partial(body, mesh.shape["blk"], mesh.shape["rep"])
    return jax.shard_map(run, mesh=mesh, in_specs=in_specs, out_specs=out_specs, check_vma=False)
```

```python
import functools
import itertools

import jax
import jax.numpy as jnp
from jax import lax
from jax.experimental import pallas as pl
from jax.experimental.pallas import tpu as pltpu
from jax.sharding import PartitionSpec as P

TILE = 128
MESH = pl.DeviceIdType.MESH


def split_of(blk_count):
    cores = 2 if blk_count % 2 == 0 else 1
    mids = 2 if (blk_count // cores) % 2 == 0 else 1
    return blk_count // (cores * mids), mids, cores


def kernel(
    blk_count, rep_count,
    x_hbm, mask_hbm, mult_hbm, wq_hbm, wv_hbm,
    out_ref,
    tgt, src, masks, mults, wq, wv, factors, queries, sums, sent, got,
    local_sems, tgt_send, tgt_recv, src_send, src_recv, tab_send, tab_recv, sum_send, sum_recv,
):
    fars, mids, cores = split_of(blk_count)
    b = lax.axis_index("blk")
    r = lax.axis_index("rep")
    core = b % cores
    mid = (b // cores) % mids
    far = b // (cores * mids)
    near = list(itertools.product(range(mids), range(cores), range(rep_count)))
    tables = list(itertools.product(range(mids), range(cores)))
    near_count = len(near)
    top = fars - 1

    def near_id(dm, dc, dr):
        m, c, q = (mid + dm) % mids, (core + dc) % cores, (r + dr) % rep_count
        return ((far * mids + m) * cores + c, q)

    def far_id(h):
        return ((h * mids + mid) * cores + core, r)

    def near_slot(dm, dc, dr):
        return near.index((-dm % mids, -dc % cores, -dr % rep_count))

    local = [
        pltpu.make_async_copy(x_hbm, src.at[far], local_sems.at[0]),
        pltpu.make_async_copy(wq_hbm, wq, local_sems.at[1]),
        pltpu.make_async_copy(wv_hbm, wv, local_sems.at[2]),
        pltpu.make_async_copy(mask_hbm, masks.at[0], local_sems.at[3]),
        pltpu.make_async_copy(mult_hbm, mults.at[0], local_sems.at[4]),
    ]
    local[0].start()
    barrier = pltpu.get_barrier_semaphore()
    for h in range(fars):
        @pl.when((h > far) | (h == far - 1))
        def _():
            pl.semaphore_signal(barrier, inc=1, device_id=far_id(h), device_id_type=MESH)
    for offset in near[1:]:
        pl.semaphore_signal(barrier, inc=1, device_id=near_id(*offset), device_id_type=MESH)
    for copy in local[1:]:
        copy.start()
    local[0].wait()
    pl.semaphore_wait(barrier, far + (far < top).astype(jnp.int32) + near_count - 1)

    own_ref = src.at[far]

    def down(h):
        return pltpu.make_async_remote_copy(
            src_ref=own_ref, dst_ref=own_ref, send_sem=src_send.at[0, h], recv_sem=src_recv.at[far],
            device_id=far_id(h), device_id_type=MESH)

    def up(h):
        return pltpu.make_async_remote_copy(
            src_ref=src.at[h], dst_ref=src.at[h], send_sem=src_send.at[1, h], recv_sem=src_recv.at[h],
            device_id=far_id(far + 1), device_id_type=MESH)

    def arrived(dst, sem):
        pltpu.make_async_copy(dst, dst, sem).wait()

    for h in range(fars - 1):
        pl.when(h < far)(down(h).start)
    pl.when(far < top)(lambda: up(far).start())

    copies = []
    for k, offset in reversed(list(enumerate(near))):
        if k:
            slot = near_slot(*offset)
            copies.append(pltpu.make_async_remote_copy(
                src_ref=own_ref, dst_ref=tgt.at[slot],
                send_sem=tgt_send.at[k], recv_sem=tgt_recv.at[slot],
                device_id=near_id(*offset), device_id_type=MESH))
    for k, (dm, dc) in enumerate(tables):
        if k:
            slot = tables.index((-dm % mids, -dc % cores))
            for n, (table, slots) in enumerate(((mask_hbm, masks), (mult_hbm, mults))):
                copies.append(pltpu.make_async_remote_copy(
                    src_ref=table, dst_ref=slots.at[slot],
                    send_sem=tab_send.at[n, k], recv_sem=tab_recv.at[n, slot],
                    device_id=near_id(dm, dc, 0), device_id_type=MESH))
    for copy in copies:
        copy.start()

    for h in reversed(range(fars - 1)):
        @pl.when((h < far) & (far < top))
        def _():
            arrived(src.at[h], src_recv.at[h])
            up(h).start()

    for copy in local[1:]:
        copy.wait()
    root_scale = 1.0 / x_hbm.shape[1] ** 0.5
    width = fars * TILE
    tile_count = masks.shape[2]

    def query_of(rows):
        return jnp.dot(rows, wq[...], preferred_element_type=jnp.float32).astype(jnp.bfloat16)

    def weigh(query, source, factor):
        score = lax.dot_general(query, source, (((1,), (1,)), ((), ())),
                                preferred_element_type=jnp.float32)
        score = score * factor
        return jnp.maximum(score, 0.2 * score).astype(jnp.bfloat16)

    place = lax.broadcasted_iota(jnp.int32, (tile_count, width), 1) // TILE
    tile = ((place * mids + mid) * cores + core) * rep_count + r
    one_hot = lax.broadcasted_iota(jnp.int32, (tile_count, width), 0) == tile
    one_hot = one_hot.astype(jnp.float32).astype(jnp.bfloat16)
    for k, (dm, dc) in enumerate(tables):
        if k:
            arrived(masks.at[k], tab_recv.at[0, k])
            arrived(mults.at[k], tab_recv.at[1, k])
        fac = (masks[k] * mults[k]).astype(jnp.float32).astype(jnp.bfloat16)
        wide = jnp.dot(fac, one_hot, preferred_element_type=jnp.float32) * root_scale
        rows = lax.broadcasted_iota(jnp.int32, wide.shape, 0)
        for dr in range(rep_count):
            row = jnp.sum(jnp.where(rows == (r + dr) % rep_count, wide, 0.0), axis=0, keepdims=True)
            for h in range(fars):
                factors[near.index((dm, dc, dr)), h] = row[:, h * TILE:(h + 1) * TILE]

    own = src[far]
    for k in range(near_count):
        if k:
            arrived(tgt.at[k], tgt_recv.at[k])
            rows = tgt[k]
        else:
            rows = own
        query = query_of(rows)
        queries[k] = query
        sums[k] = jnp.dot(weigh(query, own, factors[k, far]), own,
                          preferred_element_type=jnp.float32)

    at_top = (far == top).astype(jnp.int32)
    last = (1 - at_top) * top

    def await_source(h):
        @pl.when((h > far) | (far == top))
        def _():
            arrived(src.at[h], src_recv.at[h])

    rest = []
    for i in range(fars - 2):
        past = (i >= far).astype(jnp.int32)
        rest.append(i + at_top + (1 - at_top) * past)
    if rest:
        for h in rest:
            await_source(h)
        others = jnp.concatenate([src[h] for h in rest], axis=0)
        for k in range(near_count):
            factor = jnp.concatenate([factors[k, h] for h in rest], axis=1)
            sums[k] += jnp.dot(weigh(queries[k], others, factor), others,
                               preferred_element_type=jnp.float32)
    if fars > 1:
        await_source(last)
    final = src[last]
    order = sorted(range(near_count), key=lambda k: (k == 0, -sum(v > 0 for v in near[k])))
    for k in order:
        part = sums[k]
        if fars > 1:
            w = weigh(queries[k], final, factors[k, last])
            part = part + jnp.dot(w, final, preferred_element_type=jnp.float32)
        if k:
            sent[k] = part.astype(jnp.bfloat16)
            slot = near_slot(*near[k])
            copy = pltpu.make_async_remote_copy(
                src_ref=sent.at[k], dst_ref=got.at[slot],
                send_sem=sum_send.at[k], recv_sem=sum_recv.at[slot],
                device_id=near_id(*near[k]), device_id_type=MESH)
            copy.start()
            copies.append(copy)
        else:
            total = part
    for k in range(1, near_count):
        arrived(got.at[k], sum_recv.at[k])
        total = total + got[k].astype(jnp.float32)
    verts = TILE * blk_count * rep_count
    aggregate = (total * (2.0 * verts) ** (-0.5)).astype(jnp.bfloat16)
    mixed = jnp.dot(aggregate, wv[...], preferred_element_type=jnp.float32)
    out_ref[...] = (own.astype(jnp.float32) + mixed).astype(jnp.bfloat16)
    for copy in copies:
        copy.wait_send()
    for h in range(fars - 1):
        pl.when(h < far)(down(h).wait_send)
        pl.when((h <= far) & (far < top))(up(h).wait_send)


def body(blk_count, rep_count, features, tile_mask, multiplicity, w_query, w_value):
    rows, width = features.shape
    assert rows == TILE
    fars, mids, cores = split_of(blk_count)
    near_count = mids * cores * rep_count
    table_rows, table_cols = tile_mask.shape
    dma = pltpu.SemaphoreType.DMA
    return pl.pallas_call(
        functools.partial(kernel, blk_count, rep_count),
        out_shape=pltpu.VMEM((rows, width), jnp.bfloat16),
        in_specs=[pl.BlockSpec(memory_space=pl.ANY)] * 5,
        out_specs=pl.BlockSpec(memory_space=pltpu.VMEM),
        scratch_shapes=[
            pltpu.VMEM((near_count, rows, width), jnp.bfloat16),
            pltpu.VMEM((fars, rows, width), jnp.bfloat16),
            pltpu.VMEM((mids * cores, table_rows, table_cols), jnp.int32),
            pltpu.VMEM((mids * cores, table_rows, table_cols), jnp.int32),
            pltpu.VMEM(w_query.shape, jnp.bfloat16),
            pltpu.VMEM(w_value.shape, jnp.bfloat16),
            pltpu.VMEM((near_count, fars, 1, TILE), jnp.float32),
            pltpu.VMEM((near_count, rows, width), jnp.bfloat16),
            pltpu.VMEM((near_count, rows, width), jnp.float32),
            pltpu.VMEM((near_count, rows, width), jnp.bfloat16),
            pltpu.VMEM((near_count, rows, width), jnp.bfloat16),
            dma((5,)),
            dma((near_count,)), dma((near_count,)),
            dma((2, fars)), dma((fars,)),
            dma((2, mids * cores)), dma((2, mids * cores)),
            dma((near_count,)), dma((near_count,)),
        ],
        compiler_params=pltpu.CompilerParams(collective_id=0, has_side_effects=True),
    )(features, tile_mask, multiplicity, w_query, w_value)


def solution(mesh):
    in_specs = (P(("blk", "rep"), None), P("blk", None), P("blk", None), P(), P())
    out_specs = P(("blk", "rep"), None)
    run = functools.partial(body, mesh.shape["blk"], mesh.shape["rep"])
    return jax.shard_map(run, mesh=mesh, in_specs=in_specs, out_specs=out_specs, check_vma=False)
```

```python
import functools
import itertools

import jax
import jax.numpy as jnp
from jax import lax
from jax.experimental import pallas as pl
from jax.experimental.pallas import tpu as pltpu
from jax.sharding import PartitionSpec as P

TILE = 128
MESH = pl.DeviceIdType.MESH


def split_of(blk_count):
    cores = 2 if blk_count % 2 == 0 else 1
    mids = 2 if (blk_count // cores) % 2 == 0 else 1
    return blk_count // (cores * mids), mids, cores


def kernel(
    blk_count, rep_count,
    x_hbm, mask_hbm, mult_hbm, wq_hbm, wv_hbm,
    out_ref,
    tgt, src, masks, mults, wq, wv, factors, queries, sums, sent, got,
    local_sems, tgt_send, tgt_recv, src_send, src_recv, side_send, side_recv, tab_send, tab_recv, sum_send, sum_recv,
):
    fars, mids, cores = split_of(blk_count)
    b = lax.axis_index("blk")
    r = lax.axis_index("rep")
    core = b % cores
    mid = (b // cores) % mids
    far = b // (cores * mids)
    near = list(itertools.product(range(mids), range(rep_count)))
    near_count = len(near)
    top = fars - 1

    def near_id(dm, dr):
        return ((far * mids + (mid + dm) % mids) * cores + core, (r + dr) % rep_count)

    def far_id(h):
        return ((h * mids + mid) * cores + core, r)

    def near_slot(dm, dr):
        return near.index((-dm % mids, -dr % rep_count))

    sides = cores - 1
    side_id = ((far * mids + mid) * cores + (core + 1) % cores, r)

    local = [
        pltpu.make_async_copy(x_hbm, src.at[far], local_sems.at[0]),
        pltpu.make_async_copy(wq_hbm, wq, local_sems.at[1]),
        pltpu.make_async_copy(wv_hbm, wv, local_sems.at[2]),
        pltpu.make_async_copy(mask_hbm, masks.at[0], local_sems.at[3]),
        pltpu.make_async_copy(mult_hbm, mults.at[0], local_sems.at[4]),
    ]
    local[0].start()
    barrier = pltpu.get_barrier_semaphore()
    for h in range(fars):
        @pl.when((h > far) | (h == far - 1))
        def _():
            pl.semaphore_signal(barrier, inc=1, device_id=far_id(h), device_id_type=MESH)
    for offset in near[1:]:
        pl.semaphore_signal(barrier, inc=1, device_id=near_id(*offset), device_id_type=MESH)
    if sides:
        pl.semaphore_signal(barrier, inc=1, device_id=side_id, device_id_type=MESH)
    for copy in local[1:]:
        copy.start()
    local[0].wait()
    pl.semaphore_wait(barrier, far + (far < top).astype(jnp.int32) + near_count - 1 + sides)

    own_ref = src.at[far]

    def down(h):
        return pltpu.make_async_remote_copy(
            src_ref=own_ref, dst_ref=own_ref, send_sem=src_send.at[0, h], recv_sem=src_recv.at[far],
            device_id=far_id(h), device_id_type=MESH)

    def up(h):
        return pltpu.make_async_remote_copy(
            src_ref=src.at[h], dst_ref=src.at[h], send_sem=src_send.at[1, h], recv_sem=src_recv.at[h],
            device_id=far_id(far + 1), device_id_type=MESH)

    def side(h):
        return pltpu.make_async_remote_copy(
            src_ref=src.at[h], dst_ref=src.at[fars + h], send_sem=side_send.at[h],
            recv_sem=side_recv.at[h], device_id=side_id, device_id_type=MESH)

    def arrived(dst, sem):
        pltpu.make_async_copy(dst, dst, sem).wait()

    for h in range(fars - 1):
        pl.when(h < far)(down(h).start)
    pl.when(far < top)(lambda: up(far).start())

    copies = []
    for k, offset in reversed(list(enumerate(near))):
        if k:
            slot = near_slot(*offset)
            copies.append(pltpu.make_async_remote_copy(
                src_ref=own_ref, dst_ref=tgt.at[slot],
                send_sem=tgt_send.at[k], recv_sem=tgt_recv.at[slot],
                device_id=near_id(*offset), device_id_type=MESH))
    for k in range(mids):
        if k:
            slot = -k % mids
            for n, (table, slots) in enumerate(((mask_hbm, masks), (mult_hbm, mults))):
                copies.append(pltpu.make_async_remote_copy(
                    src_ref=table, dst_ref=slots.at[slot],
                    send_sem=tab_send.at[n, k], recv_sem=tab_recv.at[n, slot],
                    device_id=near_id(k, 0), device_id_type=MESH))
    for copy in copies:
        copy.start()

    if sides:
        side(far).start()
    at_top = (far == top).astype(jnp.int32)
    last = (1 - at_top) * top
    rest = []
    for i in range(fars - 2):
        below = (i < far).astype(jnp.int32)
        h = below * (far - 1 - i) + (1 - below) * (i + 1)
        rest.append(h)
        arrived(src.at[h], src_recv.at[h])
        pl.when((i < far) & (far < top))(up(h).start)
        if sides:
            side(h).start()

    for copy in local[1:]:
        copy.wait()
    root_scale = 1.0 / x_hbm.shape[1] ** 0.5
    width = cores * fars * TILE
    tile_count = masks.shape[2]

    def query_of(rows):
        return jnp.dot(rows, wq[...], preferred_element_type=jnp.float32).astype(jnp.bfloat16)

    def weigh(query, source, factor):
        score = lax.dot_general(query, source, (((1,), (1,)), ((), ())),
                                preferred_element_type=jnp.float32)
        score = score * factor
        return jnp.maximum(score, 0.2 * score).astype(jnp.bfloat16)

    place = lax.broadcasted_iota(jnp.int32, (tile_count, width), 1) // TILE
    place_core = (core + place // fars) % cores
    tile = ((place % fars * mids + mid) * cores + place_core) * rep_count + r
    one_hot = lax.broadcasted_iota(jnp.int32, (tile_count, width), 0) == tile
    one_hot = one_hot.astype(jnp.float32).astype(jnp.bfloat16)
    for k in range(mids):
        if k:
            arrived(masks.at[k], tab_recv.at[0, k])
            arrived(mults.at[k], tab_recv.at[1, k])
        fac = (masks[k] * mults[k]).astype(jnp.float32).astype(jnp.bfloat16)
        wide = jnp.dot(fac, one_hot, preferred_element_type=jnp.float32) * root_scale
        rows = lax.broadcasted_iota(jnp.int32, wide.shape, 0)
        for dr in range(rep_count):
            row = jnp.sum(jnp.where(rows == (r + dr) % rep_count, wide, 0.0), axis=0, keepdims=True)
            for h in range(cores * fars):
                factors[near.index((k, dr)), h] = row[:, h * TILE:(h + 1) * TILE]

    own = src[far]
    early = [far] + rest
    if sides:
        for h in early:
            arrived(src.at[fars + h], side_recv.at[h])
        early = early + [fars + h for h in early]
    sources = jnp.concatenate([src[h] for h in early], axis=0)
    for k in range(near_count):
        if k:
            arrived(tgt.at[k], tgt_recv.at[k])
            rows = tgt[k]
        else:
            rows = own
        query = query_of(rows)
        queries[k] = query
        factor = jnp.concatenate([factors[k, h] for h in early], axis=1)
        sums[k] = jnp.dot(weigh(query, sources, factor), sources, preferred_element_type=jnp.float32)

    if fars > 1:
        arrived(src.at[last], src_recv.at[last])
        if sides:
            side(last).start()
            first = src[last]
            for k in range(near_count):
                sums[k] += jnp.dot(weigh(queries[k], first, factors[k, last]), first,
                                   preferred_element_type=jnp.float32)
            arrived(src.at[fars + last], side_recv.at[last])
    last = last + sides * fars
    final = src[last]
    order = sorted(range(near_count), key=lambda k: (k == 0, -sum(v > 0 for v in near[k])))
    for k in order:
        part = sums[k]
        if fars > 1:
            w = weigh(queries[k], final, factors[k, last])
            part = part + jnp.dot(w, final, preferred_element_type=jnp.float32)
        if k:
            sent[k] = part.astype(jnp.bfloat16)
            slot = near_slot(*near[k])
            copy = pltpu.make_async_remote_copy(
                src_ref=sent.at[k], dst_ref=got.at[slot],
                send_sem=sum_send.at[k], recv_sem=sum_recv.at[slot],
                device_id=near_id(*near[k]), device_id_type=MESH)
            copy.start()
            copies.append(copy)
        else:
            total = part
    for k in range(1, near_count):
        arrived(got.at[k], sum_recv.at[k])
        total = total + got[k].astype(jnp.float32)
    verts = TILE * blk_count * rep_count
    aggregate = (total * (2.0 * verts) ** (-0.5)).astype(jnp.bfloat16)
    mixed = jnp.dot(aggregate, wv[...], preferred_element_type=jnp.float32)
    out_ref[...] = (own.astype(jnp.float32) + mixed).astype(jnp.bfloat16)
    for copy in copies:
        copy.wait_send()
    for h in range(fars - 1):
        pl.when(h < far)(down(h).wait_send)
        pl.when((h <= far) & (far < top))(up(h).wait_send)
    if sides:
        for h in range(fars):
            side(h).wait_send()


def body(blk_count, rep_count, features, tile_mask, multiplicity, w_query, w_value):
    rows, width = features.shape
    assert rows == TILE
    fars, mids, cores = split_of(blk_count)
    near_count = mids * rep_count
    table_rows, table_cols = tile_mask.shape
    dma = pltpu.SemaphoreType.DMA
    return pl.pallas_call(
        functools.partial(kernel, blk_count, rep_count),
        out_shape=pltpu.VMEM((rows, width), jnp.bfloat16),
        in_specs=[pl.BlockSpec(memory_space=pl.ANY)] * 5,
        out_specs=pl.BlockSpec(memory_space=pltpu.VMEM),
        scratch_shapes=[
            pltpu.VMEM((near_count, rows, width), jnp.bfloat16),
            pltpu.VMEM((cores * fars, rows, width), jnp.bfloat16),
            pltpu.VMEM((mids, table_rows, table_cols), jnp.int32),
            pltpu.VMEM((mids, table_rows, table_cols), jnp.int32),
            pltpu.VMEM(w_query.shape, jnp.bfloat16),
            pltpu.VMEM(w_value.shape, jnp.bfloat16),
            pltpu.VMEM((near_count, cores * fars, 1, TILE), jnp.float32),
            pltpu.VMEM((near_count, rows, width), jnp.bfloat16),
            pltpu.VMEM((near_count, rows, width), jnp.float32),
            pltpu.VMEM((near_count, rows, width), jnp.bfloat16),
            pltpu.VMEM((near_count, rows, width), jnp.bfloat16),
            dma((5,)),
            dma((near_count,)), dma((near_count,)),
            dma((2, fars)), dma((fars,)),
            dma((fars,)), dma((fars,)),
            dma((2, mids)), dma((2, mids)),
            dma((near_count,)), dma((near_count,)),
        ],
        compiler_params=pltpu.CompilerParams(collective_id=0, has_side_effects=True),
    )(features, tile_mask, multiplicity, w_query, w_value)


def solution(mesh):
    in_specs = (P(("blk", "rep"), None), P("blk", None), P("blk", None), P(), P())
    out_specs = P(("blk", "rep"), None)
    run = functools.partial(body, mesh.shape["blk"], mesh.shape["rep"])
    return jax.shard_map(run, mesh=mesh, in_specs=in_specs, out_specs=out_specs, check_vma=False)
```

```python
import functools
import itertools

import jax
import jax.numpy as jnp
from jax import lax
from jax.experimental import pallas as pl
from jax.experimental.pallas import tpu as pltpu
from jax.sharding import PartitionSpec as P

TILE = 128
MESH = pl.DeviceIdType.MESH


def split_of(blk_count):
    cores = 2 if blk_count % 2 == 0 else 1
    mids = 2 if (blk_count // cores) % 2 == 0 else 1
    return blk_count // (cores * mids), mids, cores


def kernel(
    blk_count, rep_count,
    x_hbm, mask_hbm, mult_hbm, wq_hbm, wv_hbm,
    out_ref,
    src, masks, mults, wq, wv, factors, queries, sums, sent, got,
    local_sems, tgt_send, tgt_recv, src_send, src_recv, side_send, side_recv, tab_send, tab_recv, sum_send, sum_recv,
):
    fars, mids, cores = split_of(blk_count)
    b = lax.axis_index("blk")
    r = lax.axis_index("rep")
    core = b % cores
    mid = (b // cores) % mids
    far = b // (cores * mids)
    near = list(itertools.product(range(mids), range(rep_count)))
    near_count = len(near)
    top = fars - 1

    def near_id(dm, dr):
        return ((far * mids + (mid + dm) % mids) * cores + core, (r + dr) % rep_count)

    def far_id(h):
        return ((h * mids + mid) * cores + core, r)

    def near_slot(dm, dr):
        return near.index((-dm % mids, -dr % rep_count))

    sides = cores - 1
    side_id = ((far * mids + mid) * cores + (core + 1) % cores, r)

    local = [
        pltpu.make_async_copy(x_hbm, src.at[far], local_sems.at[0]),
        pltpu.make_async_copy(wq_hbm, wq, local_sems.at[1]),
        pltpu.make_async_copy(wv_hbm, wv, local_sems.at[2]),
        pltpu.make_async_copy(mask_hbm, masks.at[0], local_sems.at[3]),
        pltpu.make_async_copy(mult_hbm, mults.at[0], local_sems.at[4]),
    ]
    local[0].start()
    barrier = pltpu.get_barrier_semaphore()
    for h in range(fars):
        @pl.when((h > far) | (h == far - 1))
        def _():
            pl.semaphore_signal(barrier, inc=1, device_id=far_id(h), device_id_type=MESH)
    for offset in near[1:]:
        pl.semaphore_signal(barrier, inc=1, device_id=near_id(*offset), device_id_type=MESH)
    if sides:
        pl.semaphore_signal(barrier, inc=1, device_id=side_id, device_id_type=MESH)
    for copy in local[1:]:
        copy.start()
    local[0].wait()
    local[1].wait()
    queries[0] = jnp.dot(src[far], wq[...], preferred_element_type=jnp.float32).astype(jnp.bfloat16)
    pl.semaphore_wait(barrier, far + (far < top).astype(jnp.int32) + near_count - 1 + sides)

    own_ref = src.at[far]

    def down(h):
        return pltpu.make_async_remote_copy(
            src_ref=own_ref, dst_ref=own_ref, send_sem=src_send.at[0, h], recv_sem=src_recv.at[far],
            device_id=far_id(h), device_id_type=MESH)

    def up(h):
        return pltpu.make_async_remote_copy(
            src_ref=src.at[h], dst_ref=src.at[h], send_sem=src_send.at[1, h], recv_sem=src_recv.at[h],
            device_id=far_id(far + 1), device_id_type=MESH)

    def side(h):
        return pltpu.make_async_remote_copy(
            src_ref=src.at[h], dst_ref=src.at[fars + h], send_sem=side_send.at[h],
            recv_sem=side_recv.at[h], device_id=side_id, device_id_type=MESH)

    def arrived(dst, sem):
        pltpu.make_async_copy(dst, dst, sem).wait()

    for h in range(fars - 1):
        pl.when(h < far)(down(h).start)
    pl.when(far < top)(lambda: up(far).start())

    copies = []
    for k, offset in reversed(list(enumerate(near))):
        if k:
            slot = near_slot(*offset)
            copies.append(pltpu.make_async_remote_copy(
                src_ref=queries.at[0], dst_ref=queries.at[slot],
                send_sem=tgt_send.at[k], recv_sem=tgt_recv.at[slot],
                device_id=near_id(*offset), device_id_type=MESH))
    for k in range(mids):
        if k:
            slot = -k % mids
            for n, (table, slots) in enumerate(((mask_hbm, masks), (mult_hbm, mults))):
                copies.append(pltpu.make_async_remote_copy(
                    src_ref=table, dst_ref=slots.at[slot],
                    send_sem=tab_send.at[n, k], recv_sem=tab_recv.at[n, slot],
                    device_id=near_id(k, 0), device_id_type=MESH))
    for copy in copies:
        copy.start()

    if sides:
        side(far).start()
    at_top = (far == top).astype(jnp.int32)
    last = (1 - at_top) * top
    rest = []
    for i in range(fars - 2):
        below = (i < far).astype(jnp.int32)
        h = below * (far - 1 - i) + (1 - below) * (i + 1)
        rest.append(h)
        arrived(src.at[h], src_recv.at[h])
        pl.when((i < far) & (far < top))(up(h).start)
        if sides:
            side(h).start()

    for copy in local[2:]:
        copy.wait()
    root_scale = 1.0 / x_hbm.shape[1] ** 0.5
    width = cores * fars * TILE
    tile_count = masks.shape[2]

    def times(blocks, slots):
        source = jnp.concatenate([src[h] for h in slots], axis=0)
        query = queries[blocks].reshape(-1, source.shape[1])
        score = lax.dot_general(query, source, (((1,), (1,)), ((), ())),
                                preferred_element_type=jnp.float32)
        factor = jnp.concatenate([factors[blocks, h] for h in slots], axis=2)
        score = score.reshape(factor.shape[0], TILE, source.shape[0]) * factor
        score = jnp.maximum(score, 0.2 * score).astype(jnp.bfloat16)
        part = jnp.dot(score.reshape(-1, source.shape[0]), source, preferred_element_type=jnp.float32)
        return part.reshape(factor.shape[0], TILE, source.shape[1])

    place = lax.broadcasted_iota(jnp.int32, (tile_count, width), 1) // TILE
    place_core = (core + place // fars) % cores
    tile = ((place % fars * mids + mid) * cores + place_core) * rep_count + r
    one_hot = lax.broadcasted_iota(jnp.int32, (tile_count, width), 0) == tile
    one_hot = one_hot.astype(jnp.float32).astype(jnp.bfloat16)
    for k in range(mids):
        if k:
            arrived(masks.at[k], tab_recv.at[0, k])
            arrived(mults.at[k], tab_recv.at[1, k])
        fac = (masks[k] * mults[k]).astype(jnp.float32).astype(jnp.bfloat16)
        wide = jnp.dot(fac, one_hot, preferred_element_type=jnp.float32) * root_scale
        rows = lax.broadcasted_iota(jnp.int32, wide.shape, 0)
        for dr in range(rep_count):
            row = jnp.sum(jnp.where(rows == (r + dr) % rep_count, wide, 0.0), axis=0, keepdims=True)
            for h in range(cores * fars):
                factors[near.index((k, dr)), h] = row[:, h * TILE:(h + 1) * TILE]

    own = src[far]
    early = [far] + rest
    if sides:
        for h in early:
            arrived(src.at[fars + h], side_recv.at[h])
        early = early + [fars + h for h in early]
    sums[:1] = times(slice(0, 1), early)
    for k in range(1, near_count):
        arrived(queries.at[k], tgt_recv.at[k])
    if near_count > 1:
        sums[1:] = times(slice(1, near_count), early)

    if fars > 1:
        arrived(src.at[last], src_recv.at[last])
        if sides:
            side(last).start()
            sums[...] += times(slice(0, near_count), [last])
            arrived(src.at[fars + last], side_recv.at[last])
    last = last + sides * fars
    parts = sums[...]
    if fars > 1:
        parts = parts + times(slice(0, near_count), [last])
    order = sorted(range(near_count), key=lambda k: (k == 0, -sum(v > 0 for v in near[k])))
    sent[...] = parts.astype(jnp.bfloat16)
    total = parts[0]
    for k in order:
        if k:
            slot = near_slot(*near[k])
            copy = pltpu.make_async_remote_copy(
                src_ref=sent.at[k], dst_ref=got.at[slot],
                send_sem=sum_send.at[k], recv_sem=sum_recv.at[slot],
                device_id=near_id(*near[k]), device_id_type=MESH)
            copy.start()
            copies.append(copy)
    for k in range(1, near_count):
        arrived(got.at[k], sum_recv.at[k])
        total = total + got[k].astype(jnp.float32)
    verts = TILE * blk_count * rep_count
    aggregate = (total * (2.0 * verts) ** (-0.5)).astype(jnp.bfloat16)
    mixed = jnp.dot(aggregate, wv[...], preferred_element_type=jnp.float32)
    out_ref[...] = (own.astype(jnp.float32) + mixed).astype(jnp.bfloat16)
    for copy in copies:
        copy.wait_send()
    for h in range(fars - 1):
        pl.when(h < far)(down(h).wait_send)
        pl.when((h <= far) & (far < top))(up(h).wait_send)
    if sides:
        for h in range(fars):
            side(h).wait_send()


def body(blk_count, rep_count, features, tile_mask, multiplicity, w_query, w_value):
    rows, width = features.shape
    assert rows == TILE
    fars, mids, cores = split_of(blk_count)
    near_count = mids * rep_count
    table_rows, table_cols = tile_mask.shape
    dma = pltpu.SemaphoreType.DMA
    return pl.pallas_call(
        functools.partial(kernel, blk_count, rep_count),
        out_shape=pltpu.VMEM((rows, width), jnp.bfloat16),
        in_specs=[pl.BlockSpec(memory_space=pl.ANY)] * 5,
        out_specs=pl.BlockSpec(memory_space=pltpu.VMEM),
        scratch_shapes=[
            pltpu.VMEM((cores * fars, rows, width), jnp.bfloat16),
            pltpu.VMEM((mids, table_rows, table_cols), jnp.int32),
            pltpu.VMEM((mids, table_rows, table_cols), jnp.int32),
            pltpu.VMEM(w_query.shape, jnp.bfloat16),
            pltpu.VMEM(w_value.shape, jnp.bfloat16),
            pltpu.VMEM((near_count, cores * fars, 1, TILE), jnp.float32),
            pltpu.VMEM((near_count, rows, width), jnp.bfloat16),
            pltpu.VMEM((near_count, rows, width), jnp.float32),
            pltpu.VMEM((near_count, rows, width), jnp.bfloat16),
            pltpu.VMEM((near_count, rows, width), jnp.bfloat16),
            dma((5,)),
            dma((near_count,)), dma((near_count,)),
            dma((2, fars)), dma((fars,)),
            dma((fars,)), dma((fars,)),
            dma((2, mids)), dma((2, mids)),
            dma((near_count,)), dma((near_count,)),
        ],
        compiler_params=pltpu.CompilerParams(collective_id=0, has_side_effects=True),
    )(features, tile_mask, multiplicity, w_query, w_value)


def solution(mesh):
    in_specs = (P(("blk", "rep"), None), P("blk", None), P("blk", None), P(), P())
    out_specs = P(("blk", "rep"), None)
    run = functools.partial(body, mesh.shape["blk"], mesh.shape["rep"])
    return jax.shard_map(run, mesh=mesh, in_specs=in_specs, out_specs=out_specs, check_vma=False)
```

```python
import functools
import itertools

import jax
import jax.numpy as jnp
from jax import lax
from jax.experimental import pallas as pl
from jax.experimental.pallas import tpu as pltpu
from jax.sharding import PartitionSpec as P

TILE = 128
MESH = pl.DeviceIdType.MESH


def split_of(blk_count):
    cores = 2 if blk_count % 2 == 0 else 1
    mids = 2 if (blk_count // cores) % 2 == 0 else 1
    return blk_count // (cores * mids), mids, cores


def kernel(
    blk_count, rep_count,
    x_hbm, mask_hbm, mult_hbm, wq_hbm, wv_hbm,
    out_ref,
    src, masks, mults, wq, wv, factors, queries, sums, sent, got,
    local_sems, tgt_send, tgt_recv, src_send, src_recv, side_send, side_recv, tab_send, tab_recv, sum_send, sum_recv, row_sem,
):
    fars, mids, cores = split_of(blk_count)
    b = lax.axis_index("blk")
    r = lax.axis_index("rep")
    core = b % cores
    mid = (b // cores) % mids
    far = b // (cores * mids)
    near = list(itertools.product(range(mids), range(rep_count)))
    near_count = len(near)
    direct = [(dm, dr) for dm, dr in near if (dm == 0) != (dr == 0)]
    crossed = [(dm, dr) for dm, dr in near if dm and dr]
    top = fars - 1

    def near_id(dm, dr):
        return ((far * mids + (mid + dm) % mids) * cores + core, (r + dr) % rep_count)

    def far_id(h):
        return ((h * mids + mid) * cores + core, r)

    def near_slot(dm, dr):
        return near.index((-dm % mids, -dr % rep_count))

    sides = cores - 1
    side_id = ((far * mids + mid) * cores + (core + 1) % cores, r)

    local = [
        pltpu.make_async_copy(x_hbm, src.at[far], local_sems.at[0]),
        pltpu.make_async_copy(wq_hbm, wq, local_sems.at[1]),
        pltpu.make_async_copy(wv_hbm, wv, local_sems.at[2]),
        pltpu.make_async_copy(mask_hbm, masks.at[0], local_sems.at[3]),
        pltpu.make_async_copy(mult_hbm, mults.at[0], local_sems.at[4]),
    ]
    local[0].start()
    barrier = pltpu.get_barrier_semaphore()
    for h in range(fars):
        @pl.when((h > far) | (h == far - 1))
        def _():
            pl.semaphore_signal(barrier, inc=1, device_id=far_id(h), device_id_type=MESH)
    for offset in direct:
        pl.semaphore_signal(barrier, inc=1, device_id=near_id(*offset), device_id_type=MESH)
    if sides:
        pl.semaphore_signal(barrier, inc=1, device_id=side_id, device_id_type=MESH)
    for copy in local[1:]:
        copy.start()
    local[0].wait()
    local[1].wait()
    queries[0] = jnp.dot(src[far], wq[...], preferred_element_type=jnp.float32).astype(jnp.bfloat16)
    pl.semaphore_wait(barrier, far + (far < top).astype(jnp.int32) + len(direct) + sides)
    if crossed:
        for dm in range(1, mids):
            pl.semaphore_signal(row_sem, inc=1, device_id=near_id(dm, 0), device_id_type=MESH)

    own_ref = src.at[far]

    def down(h):
        return pltpu.make_async_remote_copy(
            src_ref=own_ref, dst_ref=own_ref, send_sem=src_send.at[0, h], recv_sem=src_recv.at[far],
            device_id=far_id(h), device_id_type=MESH)

    def up(h):
        return pltpu.make_async_remote_copy(
            src_ref=src.at[h], dst_ref=src.at[h], send_sem=src_send.at[1, h], recv_sem=src_recv.at[h],
            device_id=far_id(far + 1), device_id_type=MESH)

    def side(h):
        return pltpu.make_async_remote_copy(
            src_ref=src.at[h], dst_ref=src.at[fars + h], send_sem=side_send.at[h],
            recv_sem=side_recv.at[h], device_id=side_id, device_id_type=MESH)

    def arrived(dst, sem):
        pltpu.make_async_copy(dst, dst, sem).wait()

    for h in range(fars - 1):
        pl.when(h < far)(down(h).start)
    pl.when(far < top)(lambda: up(far).start())

    copies = []

    def send_queries(offsets):
        for offset in offsets:
            k = near.index(offset)
            slot = near_slot(*offset)
            copies.append(pltpu.make_async_remote_copy(
                src_ref=queries.at[0], dst_ref=queries.at[slot],
                send_sem=tgt_send.at[k], recv_sem=tgt_recv.at[slot],
                device_id=near_id(*offset), device_id_type=MESH))
    for k in range(mids):
        if k:
            slot = -k % mids
            for n, (table, slots) in enumerate(((mask_hbm, masks), (mult_hbm, mults))):
                copies.append(pltpu.make_async_remote_copy(
                    src_ref=table, dst_ref=slots.at[slot],
                    send_sem=tab_send.at[n, k], recv_sem=tab_recv.at[n, slot],
                    device_id=near_id(k, 0), device_id_type=MESH))
    send_queries(direct)
    for copy in copies:
        copy.start()
    if sides:
        side(far).start()
    if crossed:
        pl.semaphore_wait(row_sem, mids - 1)
        crossed_from = len(copies)
        send_queries(crossed)
        for copy in copies[crossed_from:]:
            copy.start()
    at_top = (far == top).astype(jnp.int32)
    last = (1 - at_top) * top
    rest = []
    for i in range(fars - 2):
        below = (i < far).astype(jnp.int32)
        h = below * (far - 1 - i) + (1 - below) * (i + 1)
        rest.append(h)
        arrived(src.at[h], src_recv.at[h])
        pl.when((i < far) & (far < top))(up(h).start)
        if sides:
            side(h).start()

    for copy in local[2:]:
        copy.wait()
    root_scale = 1.0 / x_hbm.shape[1] ** 0.5
    width = cores * fars * TILE
    tile_count = masks.shape[2]

    def times(blocks, slots):
        source = jnp.concatenate([src[h] for h in slots], axis=0)
        query = queries[blocks].reshape(-1, source.shape[1])
        score = lax.dot_general(query, source, (((1,), (1,)), ((), ())),
                                preferred_element_type=jnp.float32)
        factor = jnp.concatenate([factors[blocks, h] for h in slots], axis=2)
        score = score.reshape(factor.shape[0], TILE, source.shape[0]) * factor
        score = jnp.maximum(score, 0.2 * score).astype(jnp.bfloat16)
        part = jnp.dot(score.reshape(-1, source.shape[0]), source, preferred_element_type=jnp.float32)
        return part.reshape(factor.shape[0], TILE, source.shape[1])

    place = lax.broadcasted_iota(jnp.int32, (tile_count, width), 1) // TILE
    place_core = (core + place // fars) % cores
    tile = ((place % fars * mids + mid) * cores + place_core) * rep_count + r
    one_hot = lax.broadcasted_iota(jnp.int32, (tile_count, width), 0) == tile
    one_hot = one_hot.astype(jnp.float32).astype(jnp.bfloat16)
    for k in range(mids):
        if k:
            arrived(masks.at[k], tab_recv.at[0, k])
            arrived(mults.at[k], tab_recv.at[1, k])
        fac = (masks[k] * mults[k]).astype(jnp.float32).astype(jnp.bfloat16)
        wide = jnp.dot(fac, one_hot, preferred_element_type=jnp.float32) * root_scale
        rows = lax.broadcasted_iota(jnp.int32, wide.shape, 0)
        for dr in range(rep_count):
            row = jnp.sum(jnp.where(rows == (r + dr) % rep_count, wide, 0.0), axis=0, keepdims=True)
            for h in range(cores * fars):
                factors[near.index((k, dr)), h] = row[:, h * TILE:(h + 1) * TILE]

    own = src[far]
    early = [far] + rest
    if sides:
        for h in early:
            arrived(src.at[fars + h], side_recv.at[h])
        early = early + [fars + h for h in early]
    sums[:1] = times(slice(0, 1), early)
    for k in range(1, near_count):
        arrived(queries.at[k], tgt_recv.at[k])
    if near_count > 1:
        sums[1:] = times(slice(1, near_count), early)

    if fars > 1:
        arrived(src.at[last], src_recv.at[last])
        if sides:
            side(last).start()
            sums[...] += times(slice(0, near_count), [last])
            arrived(src.at[fars + last], side_recv.at[last])
    last = last + sides * fars
    parts = sums[...]
    if fars > 1:
        parts = parts + times(slice(0, near_count), [last])
    order = sorted(range(near_count), key=lambda k: (k == 0, -sum(v > 0 for v in near[k])))
    sent[...] = parts.astype(jnp.bfloat16)
    total = parts[0]
    for k in order:
        if k:
            slot = near_slot(*near[k])
            copy = pltpu.make_async_remote_copy(
                src_ref=sent.at[k], dst_ref=got.at[slot],
                send_sem=sum_send.at[k], recv_sem=sum_recv.at[slot],
                device_id=near_id(*near[k]), device_id_type=MESH)
            copy.start()
            copies.append(copy)
    for k in range(1, near_count):
        arrived(got.at[k], sum_recv.at[k])
        total = total + got[k].astype(jnp.float32)
    verts = TILE * blk_count * rep_count
    aggregate = (total * (2.0 * verts) ** (-0.5)).astype(jnp.bfloat16)
    mixed = jnp.dot(aggregate, wv[...], preferred_element_type=jnp.float32)
    out_ref[...] = (own.astype(jnp.float32) + mixed).astype(jnp.bfloat16)
    for copy in copies:
        copy.wait_send()
    for h in range(fars - 1):
        pl.when(h < far)(down(h).wait_send)
        pl.when((h <= far) & (far < top))(up(h).wait_send)
    if sides:
        for h in range(fars):
            side(h).wait_send()


def body(blk_count, rep_count, features, tile_mask, multiplicity, w_query, w_value):
    rows, width = features.shape
    assert rows == TILE
    fars, mids, cores = split_of(blk_count)
    near_count = mids * rep_count
    table_rows, table_cols = tile_mask.shape
    dma = pltpu.SemaphoreType.DMA
    return pl.pallas_call(
        functools.partial(kernel, blk_count, rep_count),
        out_shape=pltpu.VMEM((rows, width), jnp.bfloat16),
        in_specs=[pl.BlockSpec(memory_space=pl.ANY)] * 5,
        out_specs=pl.BlockSpec(memory_space=pltpu.VMEM),
        scratch_shapes=[
            pltpu.VMEM((cores * fars, rows, width), jnp.bfloat16),
            pltpu.VMEM((mids, table_rows, table_cols), jnp.int32),
            pltpu.VMEM((mids, table_rows, table_cols), jnp.int32),
            pltpu.VMEM(w_query.shape, jnp.bfloat16),
            pltpu.VMEM(w_value.shape, jnp.bfloat16),
            pltpu.VMEM((near_count, cores * fars, 1, TILE), jnp.float32),
            pltpu.VMEM((near_count, rows, width), jnp.bfloat16),
            pltpu.VMEM((near_count, rows, width), jnp.float32),
            pltpu.VMEM((near_count, rows, width), jnp.bfloat16),
            pltpu.VMEM((near_count, rows, width), jnp.bfloat16),
            dma((5,)),
            dma((near_count,)), dma((near_count,)),
            dma((2, fars)), dma((fars,)),
            dma((fars,)), dma((fars,)),
            dma((2, mids)), dma((2, mids)),
            dma((near_count,)), dma((near_count,)),
            pltpu.SemaphoreType.REGULAR,
        ],
        compiler_params=pltpu.CompilerParams(collective_id=0, has_side_effects=True),
    )(features, tile_mask, multiplicity, w_query, w_value)


def solution(mesh):
    in_specs = (P(("blk", "rep"), None), P("blk", None), P("blk", None), P(), P())
    out_specs = P(("blk", "rep"), None)
    run = functools.partial(body, mesh.shape["blk"], mesh.shape["rep"])
    return jax.shard_map(run, mesh=mesh, in_specs=in_specs, out_specs=out_specs, check_vma=False)
```

```python
import functools
import itertools

import jax
import jax.numpy as jnp
from jax import lax
from jax.experimental import pallas as pl
from jax.experimental.pallas import tpu as pltpu
from jax.sharding import PartitionSpec as P

TILE = 128
MESH = pl.DeviceIdType.MESH


def split_of(blk_count):
    cores = 2 if blk_count % 2 == 0 else 1
    mids = 2 if (blk_count // cores) % 2 == 0 else 1
    return blk_count // (cores * mids), mids, cores


def kernel(
    blk_count, rep_count,
    x_hbm, mask_hbm, mult_hbm, wq_hbm, wv_hbm,
    out_ref,
    src, masks, mults, wq, wv, factors, queries, sums, sent, got,
    local_sems, tgt_send, tgt_recv, src_send, src_recv, side_send, side_recv, tab_send, tab_recv, sum_send, sum_recv, row_sem,
):
    fars, mids, cores = split_of(blk_count)
    b = lax.axis_index("blk")
    r = lax.axis_index("rep")
    core = b % cores
    mid = (b // cores) % mids
    far = b // (cores * mids)
    near = list(itertools.product(range(mids), range(rep_count)))
    near_count = len(near)
    direct = [(dm, dr) for dm, dr in near if (dm == 0) != (dr == 0)]
    crossed = [(dm, dr) for dm, dr in near if dm and dr]
    top = fars - 1

    def near_id(dm, dr):
        return ((far * mids + (mid + dm) % mids) * cores + core, (r + dr) % rep_count)

    def far_id(h):
        return ((h * mids + mid) * cores + core, r)

    def near_slot(dm, dr):
        return near.index((-dm % mids, -dr % rep_count))

    sides = cores - 1
    side_id = ((far * mids + mid) * cores + (core + 1) % cores, r)

    local = [
        pltpu.make_async_copy(x_hbm, src.at[far], local_sems.at[0]),
        pltpu.make_async_copy(wq_hbm, wq, local_sems.at[1]),
        pltpu.make_async_copy(wv_hbm, wv, local_sems.at[2]),
        pltpu.make_async_copy(mask_hbm, masks.at[0], local_sems.at[3]),
        pltpu.make_async_copy(mult_hbm, mults.at[0], local_sems.at[4]),
    ]
    local[0].start()
    barrier = pltpu.get_barrier_semaphore()
    for h in range(fars):
        @pl.when((h > far) | (h == far - 1))
        def _():
            pl.semaphore_signal(barrier, inc=1, device_id=far_id(h), device_id_type=MESH)
    for offset in direct:
        pl.semaphore_signal(barrier, inc=1, device_id=near_id(*offset), device_id_type=MESH)
    if sides:
        pl.semaphore_signal(barrier, inc=1, device_id=side_id, device_id_type=MESH)
    for copy in local[1:]:
        copy.start()
    local[0].wait()
    local[1].wait()
    queries[0] = jnp.dot(src[far], wq[...], preferred_element_type=jnp.float32).astype(jnp.bfloat16)
    pl.semaphore_wait(barrier, far + (far < top).astype(jnp.int32) + len(direct) + sides)
    if crossed:
        for dm in range(1, mids):
            pl.semaphore_signal(row_sem, inc=1, device_id=near_id(dm, 0), device_id_type=MESH)

    own_ref = src.at[far]

    def down(h):
        return pltpu.make_async_remote_copy(
            src_ref=own_ref, dst_ref=own_ref, send_sem=src_send.at[0, h], recv_sem=src_recv.at[far],
            device_id=far_id(h), device_id_type=MESH)

    def up(h):
        return pltpu.make_async_remote_copy(
            src_ref=src.at[h], dst_ref=src.at[h], send_sem=src_send.at[1, h], recv_sem=src_recv.at[h],
            device_id=far_id(far + 1), device_id_type=MESH)

    def side(h):
        return pltpu.make_async_remote_copy(
            src_ref=src.at[h], dst_ref=src.at[fars + h], send_sem=side_send.at[h],
            recv_sem=side_recv.at[h], device_id=side_id, device_id_type=MESH)

    hop = fars > 2

    def goes_down(h):
        return (h < far) & ((far < top) | (h != top - 2)) if hop else h < far

    def pass_down():
        return pltpu.make_async_remote_copy(
            src_ref=src.at[top], dst_ref=src.at[top], send_sem=src_send.at[0, top],
            recv_sem=src_recv.at[top], device_id=far_id(top - 2), device_id_type=MESH)

    def arrived(dst, sem):
        pltpu.make_async_copy(dst, dst, sem).wait()

    for h in range(fars - 1):
        pl.when(goes_down(h))(down(h).start)
    pl.when(far < top)(lambda: up(far).start())

    copies = []

    def send_queries(offsets):
        for offset in offsets:
            k = near.index(offset)
            slot = near_slot(*offset)
            copies.append(pltpu.make_async_remote_copy(
                src_ref=queries.at[0], dst_ref=queries.at[slot],
                send_sem=tgt_send.at[k], recv_sem=tgt_recv.at[slot],
                device_id=near_id(*offset), device_id_type=MESH))
    for k in range(mids):
        if k:
            slot = -k % mids
            for n, (table, slots) in enumerate(((mask_hbm, masks), (mult_hbm, mults))):
                copies.append(pltpu.make_async_remote_copy(
                    src_ref=table, dst_ref=slots.at[slot],
                    send_sem=tab_send.at[n, k], recv_sem=tab_recv.at[n, slot],
                    device_id=near_id(k, 0), device_id_type=MESH))
    send_queries(direct)
    for copy in copies:
        copy.start()
    if sides:
        side(far).start()
    if crossed:
        pl.semaphore_wait(row_sem, mids - 1)
        crossed_from = len(copies)
        send_queries(crossed)
        for copy in copies[crossed_from:]:
            copy.start()
    at_top = (far == top).astype(jnp.int32)
    last = (1 - at_top) * top
    rest = []
    for i in range(fars - 2):
        below = (i < far).astype(jnp.int32)
        h = below * (far - 1 - i) + (1 - below) * (i + 1)
        rest.append(h)
        arrived(src.at[h], src_recv.at[h])
        pl.when((i < far) & (far < top))(up(h).start)
        if sides:
            side(h).start()

    if hop:
        @pl.when(far == top - 1)
        def _():
            arrived(src.at[top], src_recv.at[top])
            pass_down().start()

    for copy in local[2:]:
        copy.wait()
    root_scale = 1.0 / x_hbm.shape[1] ** 0.5
    width = cores * fars * TILE
    tile_count = masks.shape[2]

    def times(blocks, slots):
        source = jnp.concatenate([src[h] for h in slots], axis=0)
        query = queries[blocks].reshape(-1, source.shape[1])
        score = lax.dot_general(query, source, (((1,), (1,)), ((), ())),
                                preferred_element_type=jnp.float32)
        factor = jnp.concatenate([factors[blocks, h] for h in slots], axis=2)
        score = score.reshape(factor.shape[0], TILE, source.shape[0]) * factor
        score = jnp.maximum(score, 0.2 * score).astype(jnp.bfloat16)
        part = jnp.dot(score.reshape(-1, source.shape[0]), source, preferred_element_type=jnp.float32)
        return part.reshape(factor.shape[0], TILE, source.shape[1])

    place = lax.broadcasted_iota(jnp.int32, (tile_count, width), 1) // TILE
    place_core = (core + place // fars) % cores
    tile = ((place % fars * mids + mid) * cores + place_core) * rep_count + r
    one_hot = lax.broadcasted_iota(jnp.int32, (tile_count, width), 0) == tile
    one_hot = one_hot.astype(jnp.float32).astype(jnp.bfloat16)
    for k in range(mids):
        if k:
            arrived(masks.at[k], tab_recv.at[0, k])
            arrived(mults.at[k], tab_recv.at[1, k])
        fac = (masks[k] * mults[k]).astype(jnp.float32).astype(jnp.bfloat16)
        wide = jnp.dot(fac, one_hot, preferred_element_type=jnp.float32) * root_scale
        rows = lax.broadcasted_iota(jnp.int32, wide.shape, 0)
        for dr in range(rep_count):
            row = jnp.sum(jnp.where(rows == (r + dr) % rep_count, wide, 0.0), axis=0, keepdims=True)
            for h in range(cores * fars):
                factors[near.index((k, dr)), h] = row[:, h * TILE:(h + 1) * TILE]

    own = src[far]
    early = [far] + rest
    if sides:
        for h in early:
            arrived(src.at[fars + h], side_recv.at[h])
        early = early + [fars + h for h in early]
    sums[:1] = times(slice(0, 1), early)
    for k in range(1, near_count):
        arrived(queries.at[k], tgt_recv.at[k])
    if near_count > 1:
        sums[1:] = times(slice(1, near_count), early)

    if fars > 1:
        if hop:
            @pl.when(far != top - 1)
            def _():
                arrived(src.at[last], src_recv.at[last])
        else:
            arrived(src.at[last], src_recv.at[last])
        if sides:
            side(last).start()
            sums[...] += times(slice(0, near_count), [last])
            arrived(src.at[fars + last], side_recv.at[last])
    last = last + sides * fars
    parts = sums[...]
    if fars > 1:
        parts = parts + times(slice(0, near_count), [last])
    order = sorted(range(near_count), key=lambda k: (k == 0, -sum(v > 0 for v in near[k])))
    sent[...] = parts.astype(jnp.bfloat16)
    total = parts[0]
    for k in order:
        if k:
            slot = near_slot(*near[k])
            copy = pltpu.make_async_remote_copy(
                src_ref=sent.at[k], dst_ref=got.at[slot],
                send_sem=sum_send.at[k], recv_sem=sum_recv.at[slot],
                device_id=near_id(*near[k]), device_id_type=MESH)
            copy.start()
            copies.append(copy)
    for k in range(1, near_count):
        arrived(got.at[k], sum_recv.at[k])
        total = total + got[k].astype(jnp.float32)
    verts = TILE * blk_count * rep_count
    aggregate = (total * (2.0 * verts) ** (-0.5)).astype(jnp.bfloat16)
    mixed = jnp.dot(aggregate, wv[...], preferred_element_type=jnp.float32)
    out_ref[...] = (own.astype(jnp.float32) + mixed).astype(jnp.bfloat16)
    for copy in copies:
        copy.wait_send()
    for h in range(fars - 1):
        pl.when(goes_down(h))(down(h).wait_send)
        pl.when((h <= far) & (far < top))(up(h).wait_send)
    if hop:
        pl.when(far == top - 1)(pass_down().wait_send)
    if sides:
        for h in range(fars):
            side(h).wait_send()


def body(blk_count, rep_count, features, tile_mask, multiplicity, w_query, w_value):
    rows, width = features.shape
    assert rows == TILE
    fars, mids, cores = split_of(blk_count)
    near_count = mids * rep_count
    table_rows, table_cols = tile_mask.shape
    dma = pltpu.SemaphoreType.DMA
    return pl.pallas_call(
        functools.partial(kernel, blk_count, rep_count),
        out_shape=pltpu.VMEM((rows, width), jnp.bfloat16),
        in_specs=[pl.BlockSpec(memory_space=pl.ANY)] * 5,
        out_specs=pl.BlockSpec(memory_space=pltpu.VMEM),
        scratch_shapes=[
            pltpu.VMEM((cores * fars, rows, width), jnp.bfloat16),
            pltpu.VMEM((mids, table_rows, table_cols), jnp.int32),
            pltpu.VMEM((mids, table_rows, table_cols), jnp.int32),
            pltpu.VMEM(w_query.shape, jnp.bfloat16),
            pltpu.VMEM(w_value.shape, jnp.bfloat16),
            pltpu.VMEM((near_count, cores * fars, 1, TILE), jnp.float32),
            pltpu.VMEM((near_count, rows, width), jnp.bfloat16),
            pltpu.VMEM((near_count, rows, width), jnp.float32),
            pltpu.VMEM((near_count, rows, width), jnp.bfloat16),
            pltpu.VMEM((near_count, rows, width), jnp.bfloat16),
            dma((5,)),
            dma((near_count,)), dma((near_count,)),
            dma((2, fars)), dma((fars,)),
            dma((fars,)), dma((fars,)),
            dma((2, mids)), dma((2, mids)),
            dma((near_count,)), dma((near_count,)),
            pltpu.SemaphoreType.REGULAR,
        ],
        compiler_params=pltpu.CompilerParams(collective_id=0, has_side_effects=True),
    )(features, tile_mask, multiplicity, w_query, w_value)


def solution(mesh):
    in_specs = (P(("blk", "rep"), None), P("blk", None), P("blk", None), P(), P())
    out_specs = P(("blk", "rep"), None)
    run = functools.partial(body, mesh.shape["blk"], mesh.shape["rep"])
    return jax.shard_map(run, mesh=mesh, in_specs=in_specs, out_specs=out_specs, check_vma=False)
```
